32 devices in a mesh: dp: 8 (over y, x, core), tensor: 4 (over z).
Axes of the slice: x: 2, y: 2, z: 4, core: 2. Of those that a mesh axis runs over, the one named last changes fastest.
Arguments:
- hidden_in: bfloat16 [4096, 1024], P(('dp', 'tensor')), may hold values from -6 to 6
- cotangent: bfloat16 [4096, 1024], P(('dp', 'tensor')), may hold values from -6 to 6
- seq_lengths: int32 [8, 3], P('dp'), may hold values from 1 to 384, 512 in all within a row
- first_gain: float32 [1024], P(('dp', 'tensor')), may hold values from 0.5 to 1.5
- first_shift: float32 [1024], P(('dp', 'tensor')), may hold values from -2 to 2
- second_gain: float32 [1024], P(('dp', 'tensor')), may hold values from 0.5 to 1.5
- second_shift: float32 [1024], P(('dp', 'tensor')), may hold values from -2 to 2
- qkv_weight: bfloat16 [1024, 3072], P('dp', 'tensor'), may hold values from -2 to 2
- qkv_bias: bfloat16 [16, 192], P('tensor', 'dp'), may hold values from -3 to 3
- dense_weight: bfloat16 [1024, 1024], P('tensor', 'dp'), may hold values from -1.5 to 1.5
- dense_bias: float32 [1024], P(('dp', 'tensor')), may hold values from -3 to 3
- up_weight: bfloat16 [1024, 4096], P('dp', 'tensor'), may hold values from -0.1875 to 0.1875
- up_bias: bfloat16 [16, 256], P('tensor', 'dp'), may hold values from -3 to 3
- down_weight: bfloat16 [4096, 1024], P('tensor', 'dp'), may hold values from -0.09375 to 0.09375
- down_bias: float32 [1024], P(('dp', 'tensor')), may hold values from -3 to 3
Outputs:
- block_out: bfloat16 [4096, 1024], P(('dp', 'tensor'))
- input_grad: bfloat16 [4096, 1024], P(('dp', 'tensor'))
- first_gain_grad: float32 [1024], P(('dp', 'tensor'))
- first_shift_grad: float32 [1024], P(('dp', 'tensor'))
- second_gain_grad: float32 [1024], P(('dp', 'tensor'))
- second_shift_grad: float32 [1024], P(('dp', 'tensor'))
- qkv_weight_grad: float32 [1024, 3072], P('dp', 'tensor')
- qkv_bias_grad: float32 [16, 192], P('tensor', 'dp')
- dense_weight_grad: float32 [1024, 1024], P('tensor', 'dp')
- dense_bias_grad: float32 [1024], P(('dp', 'tensor'))
- up_weight_grad: float32 [1024, 4096], P('dp', 'tensor')
- up_bias_grad: float32 [16, 256], P('tensor', 'dp')
- down_weight_grad: float32 [4096, 1024], P('tensor', 'dp')
- down_bias_grad: float32 [1024], P(('dp', 'tensor'))
The draws below stay inside these ranges and needn't reach their ends.
Inputs may be any that keep to these rules, and one draw needn't show every extreme that they name: `seq_lengths`: each row's 3 lengths sum to 512; the longest of every row is exactly 384.
All inputs are finite; a program needn't handle non-finite values.
Results may differ from the reference program's by a relative error of at most 0.013.
Values may be sent and summed in bfloat16 or wider, within the bound.
No kernel may reach another device: no remote copies, remote signals or barrier semaphores. Data moves between devices by JAX's collectives and lax.ppermute only.
A program may use at most 128 MiB of HBM per device.

```python
import math
import jax
import jax.numpy as jnp
import numpy as np
from jax import lax

D = 1024
HEADS = 16
FF = 4096
HD = 64
ROT = 16
SEQS = 3
GROUP = 512
MAXLEN = 384
TOKENS = 4096
N_DP = 8


def draw_qkv_weight(key, part):
    noise_key = jax.random.fold_in(key, 11)
    base = jnp.clip(jax.random.normal(noise_key, (D, HEADS, 3, HD), jnp.float32), -4.0, 4.0)
    return (base * D ** (-0.5)).reshape(D, 3 * D).astype(jnp.bfloat16)


def block_levels(stream_key, dims, split, smallest, largest):
    level, own = 1.0, jax.random.fold_in(stream_key, 6)
    for axis_at, blocks in split:
        heights = jnp.exp(jax.random.uniform(jax.random.fold_in(own, axis_at), (blocks,), jnp.float32, smallest / len(split), largest / len(split)))
        level = level * jnp.repeat(heights, dims[axis_at] // blocks).reshape([-1 if axis == axis_at else 1 for axis in range(len(dims))])
    return level


def split_up(number_of, total, limit, skew):
    weights = [(1 << 20) // math.isqrt(grade ** skew) + 1 for grade in range(2, number_of + 1)]
    surplus, counts = total - limit - (number_of - 1), [1] * (number_of - 1)
    while surplus > 0:
        free = [i for i in range(number_of - 1) if counts[i] < limit]
        mass, left = sum([weights[i] for i in free]), surplus
        for i in free:
            more = min(limit - counts[i], max(1, left * weights[i] // mass), surplus)
            counts[i] = counts[i] + more
            surplus = surplus - more
    return np.array([limit] + counts)


def uneven_parts(rng, amount, total, most, lean):
    if amount == 2:
        one = jax.random.randint(rng, (), max(1, total - most), min(most, total - 1) + 1)
        return jnp.stack([one, total - one])
    tallies = jnp.asarray(split_up(amount, total, most, lean), jnp.int32)
    twos = (amount - 1) // 2
    giver, receiver = tallies[1:1 + 2 * twos:2], tallies[2:2 + 2 * twos:2]
    room = jnp.minimum(giver - 1, most - receiver)
    moved = jax.random.randint(jax.random.fold_in(rng, 1), (twos,), 0, 1 << 20) % (room + 1)
    tallies = tallies.at[1:1 + 2 * twos:2].set(giver - moved).at[2:2 + 2 * twos:2].set(receiver + moved)
    return tallies[jax.random.permutation(jax.random.fold_in(rng, 2), amount)]


def gaussian(own_key, dims, scale, bound, cuts=(), kind=jnp.bfloat16):
    values = scale * jax.random.normal(own_key, dims, jnp.float32)
    if cuts:
        values = values * block_levels(own_key, dims, cuts, -0.22, 0.18)
    return jnp.clip(values, -bound, bound).astype(kind)


def setup_inputs(seed: int = 0) -> dict:
    arg_keys = jax.random.split(jax.random.key(seed), 16)
    return {
        "hidden_in": gaussian(arg_keys[0], (TOKENS, D), 1.0, 6.0, ((0, 32),)),
        "cotangent": gaussian(arg_keys[1], (TOKENS, D), 1.0, 6.0, ((0, 32),)),
        "seq_lengths": jax.vmap(lambda own: uneven_parts(own, SEQS, GROUP, MAXLEN, 2))(jax.random.split(arg_keys[2], N_DP)).reshape((N_DP, SEQS)).astype(jnp.int32),
        "first_gain": jnp.clip(1.0 + 0.1 * jax.random.normal(arg_keys[3], (D,), jnp.float32), 0.5, 1.5),
        "first_shift": gaussian(arg_keys[4], (D,), 0.3, 2.0, ((0, 32),), jnp.float32),
        "second_gain": jnp.clip(1.0 + 0.1 * jax.random.normal(arg_keys[5], (D,), jnp.float32), 0.5, 1.5),
        "second_shift": gaussian(arg_keys[6], (D,), 0.3, 2.0, ((0, 32),), jnp.float32),
        "qkv_weight": draw_qkv_weight(jax.random.fold_in(arg_keys[15], 71), 0),
        "qkv_bias": gaussian(arg_keys[8], (HEADS, 3 * HD), 0.5, 3.0, ((0, 4), (1, 8))),
        "dense_weight": gaussian(arg_keys[9], (D, D), (D // 64) ** -0.5, 1.5, ((0, 4), (1, 8))),
        "dense_bias": gaussian(arg_keys[10], (D,), 0.5, 3.0, ((0, 32),), jnp.float32),
        "up_weight": gaussian(arg_keys[11], (D, FF), D ** -0.5, 0.1875, ((0, 8), (1, 4))),
        "up_bias": gaussian(arg_keys[12], (HEADS, FF // HEADS), 0.5, 3.0, ((0, 4), (1, 8))),
        "down_weight": gaussian(arg_keys[13], (FF, D), FF ** -0.5, 0.09375, ((0, 4), (1, 8))),
        "down_bias": gaussian(arg_keys[14], (D,), 0.5, 3.0, ((0, 32),), jnp.float32),
    }


EPS = 1e-05
ROOT_HALF = 0.7071067811865476
INV_ROOT_TWO_PI = 0.3989422804014327

def gelu_value(pre_act):
    return pre_act * (0.5 * (1.0 + jax.scipy.special.erf(pre_act * ROOT_HALF)))

def gelu_slope(pre_act):
    cumul = 0.5 * (1.0 + jax.scipy.special.erf(pre_act * ROOT_HALF))
    return cumul + pre_act * INV_ROOT_TWO_PI * jnp.exp(-0.5 * pre_act * pre_act)

def layout(lengths, count):
    ends = jnp.cumsum(lengths).astype(jnp.int32)
    index = jnp.arange(count, dtype=jnp.int32)
    passed = (index[:, None] >= ends[None, :]).astype(jnp.int32)
    segment = lax.optimization_barrier(jnp.sum(passed, axis=1)).astype(jnp.int32)
    start = lax.optimization_barrier(jnp.sum(passed * lengths[None, :], axis=1)).astype(jnp.int32)
    return (segment, index - start)

def rotary_tables(positions):
    half = ROT // 2
    freq = 1.0 / 10000.0 ** (jnp.arange(half, dtype=jnp.float32) * (2.0 / ROT))
    angle = positions.astype(jnp.float32)[:, None] * freq[None, :]
    return (jnp.cos(angle)[:, None, :], jnp.sin(angle)[:, None, :])

def rotate(values, cosine, sine):
    half = ROT // 2
    lower = values[..., :half]
    upper = values[..., half:ROT]
    return jnp.concatenate([lower * cosine - upper * sine, upper * cosine + lower * sine, values[..., ROT:]], axis=-1)

def rotate_back(grads, cosine, sine):
    half = ROT // 2
    lower = grads[..., :half]
    upper = grads[..., half:ROT]
    return jnp.concatenate([lower * cosine + upper * sine, upper * cosine - lower * sine, grads[..., ROT:]], axis=-1)

def score_block(query, keys, segment):
    index = jnp.arange(segment.shape[0], dtype=jnp.int32)
    allowed = (segment[:, None] == segment[None, :]) & (index[None, :] <= index[:, None])
    scores = jnp.einsum('qhd,khd->hqk', query.astype(jnp.float32), keys.astype(jnp.float32)) * HD ** (-0.5)
    return jnp.where(allowed[None], scores, -jnp.inf)

def attend_forward(projected, segment, positions):
    count = projected.shape[0]
    heads = projected.shape[1] // (3 * HD)
    parts = projected.reshape(count, heads, 3, HD)
    cosine, sine = rotary_tables(positions)
    query = rotate(parts[:, :, 0], cosine, sine).astype(jnp.bfloat16)
    keys = rotate(parts[:, :, 1], cosine, sine).astype(jnp.bfloat16)
    values = parts[:, :, 2].astype(jnp.bfloat16)
    scores = score_block(query, keys, segment)
    row_top = lax.optimization_barrier(jnp.max(scores, axis=-1, keepdims=True))
    log_total = row_top + jnp.log(lax.optimization_barrier(jnp.sum(jnp.exp(scores - row_top), axis=-1, keepdims=True)))
    prob = jnp.exp(scores - log_total).astype(jnp.bfloat16)
    context = jnp.einsum('hqk,khd->qhd', prob.astype(jnp.float32), values.astype(jnp.float32))
    return (context.reshape(count, heads * HD).astype(jnp.bfloat16), log_total, query, keys, values)

def attend_backward(query, keys, values, log_total, grad_context, segment, positions):
    count = query.shape[0]
    heads = query.shape[1]
    scores = score_block(query, keys, segment)
    prob_f = jnp.exp(scores - log_total)
    grad_ctx = grad_context.reshape(count, heads, HD).astype(jnp.float32)
    grad_prob = jnp.einsum('qhd,khd->hqk', grad_ctx, values.astype(jnp.float32))
    delta = lax.optimization_barrier(jnp.sum(prob_f * grad_prob, axis=-1, keepdims=True))
    grad_score = (prob_f * (grad_prob - delta) * HD ** (-0.5)).astype(jnp.bfloat16).astype(jnp.float32)
    grad_query = jnp.einsum('hqk,khd->qhd', grad_score, keys.astype(jnp.float32))
    grad_key = jnp.einsum('hqk,qhd->khd', grad_score, query.astype(jnp.float32))
    prob_b = prob_f.astype(jnp.bfloat16).astype(jnp.float32)
    grad_value = jnp.einsum('hqk,qhd->khd', prob_b, grad_ctx)
    cosine, sine = rotary_tables(positions)
    stacked = jnp.stack([rotate_back(grad_query, cosine, sine), rotate_back(grad_key, cosine, sine), grad_value], axis=2)
    return stacked.reshape(count, heads * 3 * HD)

def reference(hidden_in, cotangent, seq_lengths, first_gain, first_shift, second_gain, second_shift, qkv_weight, qkv_bias, dense_weight, dense_bias, up_weight, up_bias, down_weight, down_bias):
    qkv_flat = qkv_bias.reshape(-1).astype(jnp.float32)
    up_flat = up_bias.reshape(-1).astype(jnp.float32)

    def group_step(carry, inputs):
        rows, upstream, lengths = inputs
        count = rows.shape[0]
        segment, positions = layout(lengths, count)
        rows_f = rows.astype(jnp.float32)
        mean_row = lax.optimization_barrier(jnp.mean(rows_f, axis=-1, keepdims=True))
        centred = rows_f - mean_row
        inv_std = lax.rsqrt(lax.optimization_barrier(jnp.mean(centred * centred, axis=-1, keepdims=True)) + EPS)
        normed = centred * inv_std
        first = (normed * first_gain + first_shift).astype(jnp.bfloat16)
        second = (normed * second_gain + second_shift).astype(jnp.bfloat16)
        projected = jnp.dot(first, qkv_weight, preferred_element_type=jnp.float32) + qkv_flat
        context, log_total, query, keys, values = attend_forward(projected, segment, positions)
        pre_act = jnp.dot(second, up_weight, preferred_element_type=jnp.float32) + up_flat
        active = gelu_value(pre_act).astype(jnp.bfloat16)
        attn_part = jnp.dot(context, dense_weight, preferred_element_type=jnp.float32)
        mlp_part = jnp.dot(active, down_weight, preferred_element_type=jnp.float32)
        block_out = (rows_f + attn_part + mlp_part + dense_bias + down_bias).astype(jnp.bfloat16)
        upstream_f = upstream.astype(jnp.float32)
        bias_grad = lax.optimization_barrier(jnp.sum(upstream_f, axis=0))
        down_grad = jnp.dot(active.T, upstream, preferred_element_type=jnp.float32)
        dense_grad = jnp.dot(context.T, upstream, preferred_element_type=jnp.float32)
        grad_pre = jnp.dot(upstream, down_weight.T, preferred_element_type=jnp.float32) * gelu_slope(pre_act)
        up_bias_grad = lax.optimization_barrier(jnp.sum(grad_pre, axis=0))
        grad_pre_b = grad_pre.astype(jnp.bfloat16)
        up_grad = jnp.dot(second.T, grad_pre_b, preferred_element_type=jnp.float32)
        grad_second = jnp.dot(grad_pre_b, up_weight.T, preferred_element_type=jnp.float32)
        grad_context = jnp.dot(upstream, dense_weight.T, preferred_element_type=jnp.float32).astype(jnp.bfloat16)
        grad_projected = attend_backward(query, keys, values, log_total, grad_context, segment, positions)
        qkv_bias_grad = lax.optimization_barrier(jnp.sum(grad_projected, axis=0))
        grad_projected_b = grad_projected.astype(jnp.bfloat16)
        qkv_grad = jnp.dot(first.T, grad_projected_b, preferred_element_type=jnp.float32)
        grad_first = jnp.dot(grad_projected_b, qkv_weight.T, preferred_element_type=jnp.float32)
        gain_one = lax.optimization_barrier(jnp.sum(grad_first * normed, axis=0))
        shift_one = lax.optimization_barrier(jnp.sum(grad_first, axis=0))
        gain_two = lax.optimization_barrier(jnp.sum(grad_second * normed, axis=0))
        shift_two = lax.optimization_barrier(jnp.sum(grad_second, axis=0))
        grad_normed = grad_first * first_gain + grad_second * second_gain
        mean_a = lax.optimization_barrier(jnp.mean(grad_normed, axis=-1, keepdims=True))
        mean_b = lax.optimization_barrier(jnp.mean(grad_normed * normed, axis=-1, keepdims=True))
        input_grad = (upstream_f + inv_std * (grad_normed - mean_a - normed * mean_b)).astype(jnp.bfloat16)
        grads = (gain_one, shift_one, gain_two, shift_two, qkv_grad, qkv_bias_grad, dense_grad, bias_grad, up_grad, up_bias_grad, down_grad)
        carry = jax.tree.map(lambda left, right: left + right, carry, grads)
        return (carry, (block_out, input_grad))
    init = (jnp.zeros((D,), jnp.float32), jnp.zeros((D,), jnp.float32), jnp.zeros((D,), jnp.float32), jnp.zeros((D,), jnp.float32), jnp.zeros((D, 3 * D), jnp.float32), jnp.zeros((3 * D,), jnp.float32), jnp.zeros((D, D), jnp.float32), jnp.zeros((D,), jnp.float32), jnp.zeros((D, FF), jnp.float32), jnp.zeros((FF,), jnp.float32), jnp.zeros((FF, D), jnp.float32))
    totals, (outs, in_grads) = lax.scan(group_step, init, (hidden_in.reshape(N_DP, GROUP, D), cotangent.reshape(N_DP, GROUP, D), seq_lengths))
    gain_one, shift_one, gain_two, shift_two, qkv_grad, qkv_bias_grad, dense_grad, bias_grad, up_grad, up_bias_grad, down_grad = totals
    return (outs.reshape(TOKENS, D), in_grads.reshape(TOKENS, D), gain_one, shift_one, gain_two, shift_two, qkv_grad, qkv_bias_grad.reshape(HEADS, 3 * HD), dense_grad, bias_grad, up_grad, up_bias_grad.reshape(HEADS, FF // HEADS), down_grad, bias_grad)
```

```python
import functools

import jax
import jax.numpy as jnp
from jax import lax
from jax.sharding import PartitionSpec as P

HD = 64
ROT = 16


EPS = 1e-05
ROOT_HALF = 0.7071067811865476
INV_ROOT_TWO_PI = 0.3989422804014327


def gelu_value(pre_act):
    return pre_act * (0.5 * (1.0 + jax.scipy.special.erf(pre_act * ROOT_HALF)))


def gelu_slope(pre_act):
    cumul = 0.5 * (1.0 + jax.scipy.special.erf(pre_act * ROOT_HALF))
    return cumul + pre_act * INV_ROOT_TWO_PI * jnp.exp(-0.5 * pre_act * pre_act)


def layout(lengths, count):
    ends = jnp.cumsum(lengths)
    index = jnp.arange(count, dtype=jnp.int32)
    passed = (index[:, None] >= ends[None, :]).astype(jnp.int32)
    segment = jnp.sum(passed, axis=1)
    start = jnp.sum(passed * lengths[None, :], axis=1)
    return (segment, index - start)


def rotary_tables(positions):
    half = ROT // 2
    freq = 1.0 / 10000.0 ** (jnp.arange(half, dtype=jnp.float32) * (2.0 / ROT))
    angle = positions.astype(jnp.float32)[:, None] * freq[None, :]
    return (jnp.cos(angle)[:, None, :], jnp.sin(angle)[:, None, :])


def rotate(values, cosine, sine):
    half = ROT // 2
    lower = values[..., :half]
    upper = values[..., half:ROT]
    return jnp.concatenate(
        [lower * cosine - upper * sine, upper * cosine + lower * sine, values[..., ROT:]], axis=-1
    )


def rotate_back(grads, cosine, sine):
    half = ROT // 2
    lower = grads[..., :half]
    upper = grads[..., half:ROT]
    return jnp.concatenate(
        [lower * cosine + upper * sine, upper * cosine - lower * sine, grads[..., ROT:]], axis=-1
    )


def score_block(query, keys, segment):
    index = jnp.arange(segment.shape[0], dtype=jnp.int32)
    allowed = (segment[:, None] == segment[None, :]) & (index[None, :] <= index[:, None])
    scores = jnp.einsum("qhd,khd->hqk", query, keys, preferred_element_type=jnp.float32) * HD ** (
        -0.5
    )
    return jnp.where(allowed[None], scores, -jnp.inf)


def attend_forward(projected, segment, positions):
    count = projected.shape[0]
    heads = projected.shape[1] // (3 * HD)
    parts = projected.reshape(count, heads, 3, HD)
    cosine, sine = rotary_tables(positions)
    query = rotate(parts[:, :, 0], cosine, sine).astype(jnp.bfloat16)
    keys = rotate(parts[:, :, 1], cosine, sine).astype(jnp.bfloat16)
    values = parts[:, :, 2].astype(jnp.bfloat16)
    scores = score_block(query, keys, segment)
    row_top = jnp.max(scores, axis=-1, keepdims=True)
    log_total = row_top + jnp.log(jnp.sum(jnp.exp(scores - row_top), axis=-1, keepdims=True))
    prob = jnp.exp(scores - log_total).astype(jnp.bfloat16)
    context = jnp.einsum("hqk,khd->qhd", prob, values, preferred_element_type=jnp.float32)
    return (context.reshape(count, heads * HD).astype(jnp.bfloat16), log_total, query, keys, values)


def attend_backward(query, keys, values, log_total, grad_context, segment, positions):
    count = query.shape[0]
    heads = query.shape[1]
    scores = score_block(query, keys, segment)
    prob_f = jnp.exp(scores - log_total)
    grad_ctx = grad_context.reshape(count, heads, HD)
    grad_prob = jnp.einsum("qhd,khd->hqk", grad_ctx, values, preferred_element_type=jnp.float32)
    delta = jnp.sum(prob_f * grad_prob, axis=-1, keepdims=True)
    grad_score = (prob_f * (grad_prob - delta) * HD ** (-0.5)).astype(jnp.bfloat16)
    grad_query = jnp.einsum("hqk,khd->qhd", grad_score, keys, preferred_element_type=jnp.float32)
    grad_key = jnp.einsum("hqk,qhd->khd", grad_score, query, preferred_element_type=jnp.float32)
    prob_b = prob_f.astype(jnp.bfloat16)
    grad_value = jnp.einsum("hqk,qhd->khd", prob_b, grad_ctx, preferred_element_type=jnp.float32)
    cosine, sine = rotary_tables(positions)
    stacked = jnp.stack(
        [rotate_back(grad_query, cosine, sine), rotate_back(grad_key, cosine, sine), grad_value],
        axis=2,
    )
    return stacked.reshape(count, heads * 3 * HD)


def norm_stats(rows):
    rows_f = rows.astype(jnp.float32)
    mean_row = jnp.mean(rows_f, axis=-1, keepdims=True)
    centred = rows_f - mean_row
    inv_std = lax.rsqrt(jnp.mean(centred * centred, axis=-1, keepdims=True) + EPS)
    return (centred * inv_std, inv_std)


def contract_rows(left, right):
    return lax.dot_general(
        left, right, (((0,), (0,)), ((), ())), preferred_element_type=jnp.float32
    )


def contract_cols(left, right):
    return lax.dot_general(
        left, right, (((1,), (1,)), ((), ())), preferred_element_type=jnp.float32
    )


FEW = 8


def powers(count):
    return [1 << b for b in range(count.bit_length() - 1)]


def swap(value, axis, size, mask):
    return lax.ppermute(value, axis, [(i, i ^ mask) for i in range(size)])


def shuffle(pieces, masks, me):
    for mask in masks:
        flip = (me & mask) != 0
        pieces = [jnp.where(flip, pieces[k ^ mask], pieces[k]) for k in range(len(pieces))]
    return pieces


def cut(value, count, axis):
    step = value.shape[axis] // count
    return [lax.slice_in_dim(value, k * step, (k + 1) * step, axis=axis) for k in range(count)]


def gather_blocks(value, axis, size, order):
    if size > FEW:
        stack, names = value[None], [0]
        for mask in order:
            stack = jnp.concatenate([stack, swap(stack, axis, size, mask)])
            names = names + [k ^ mask for k in names]
        return [stack[names.index(k)] for k in range(size)]
    held = {0: value}
    for mask in order:
        held.update({k ^ mask: swap(held[k], axis, size, mask) for k in list(held)})
    return [held[k] for k in range(size)]


def scatter_blocks(keep, send, axis, size, order):
    first = order[0]
    if size > FEW:
        names = list(keep)
        got = swap(jnp.stack([send[k ^ first] for k in names]), axis, size, first)
        stack = jnp.stack([keep[k] for k in names]) + got.astype(jnp.float32)
        for mask in order[1:]:
            stay = [k for k in names if not k & mask]
            away = jnp.stack([stack[names.index(k ^ mask)] for k in stay]).astype(jnp.bfloat16)
            stack = jnp.stack([stack[names.index(k)] for k in stay]) + swap(
                away, axis, size, mask
            ).astype(jnp.float32)
            names = stay
        return stack[0]
    held = {k: keep[k] + swap(send[k ^ first], axis, size, first).astype(jnp.float32) for k in keep}
    for mask in order[1:]:
        held = {
            k: held[k] + swap(held[k ^ mask].astype(jnp.bfloat16), axis, size, mask).astype(jnp.float32)
            for k in held
            if not k & mask
        }
    return held[0]


def sum_blocks(blocks, axis, size, order):
    held = dict(enumerate(blocks))
    for mask in order:
        stay = [k for k in held if not k & mask]
        got = swap(jnp.stack([held[k ^ mask] for k in stay]), axis, size, mask)
        held = {k: held[k] + got[at] for at, k in enumerate(stay)}
    return held[0]


def on_device(
    n_dp,
    n_tensor,
    hidden_in,
    cotangent,
    seq_lengths,
    first_gain,
    first_shift,
    second_gain,
    second_shift,
    qkv_weight,
    qkv_bias,
    dense_weight,
    dense_bias,
    up_weight,
    up_bias,
    down_weight,
    down_bias,
):
    f32, bf16 = jnp.float32, jnp.bfloat16
    masks, z_masks = powers(n_dp), powers(n_tensor)
    high = masks[1:]
    order_a, order_b = high + masks[:1], high[::-1] + masks[:1]
    me, z_me = lax.axis_index("dp"), lax.axis_index("tensor")
    layout_order = [k for k in range(n_dp) if not k & 1] + [k for k in range(n_dp) if k & 1]

    def to_relative(value):
        pieces = shuffle(cut(value, n_dp, value.ndim - 1), masks, me)
        return jnp.concatenate([pieces[k] for k in layout_order], axis=-1)

    def from_relative(value):
        pieces = cut(value, n_dp, value.ndim - 1)
        back = [pieces[layout_order.index(k)] for k in range(n_dp)]
        return jnp.concatenate(shuffle(back, masks, me), axis=-1)

    def tokens_full(value):
        pieces = [value] + [swap(value, "tensor", n_tensor, m) for m in range(1, n_tensor)]
        return jnp.concatenate(shuffle(pieces, z_masks, z_me), axis=0)

    def tokens_sum(partial):
        count = partial.shape[0] // n_tensor
        block = lambda m: lax.dynamic_slice_in_dim(partial, (z_me ^ m) * count, count, 0)
        total = block(0)
        for m in range(1, n_tensor):
            total = total + swap(block(m).astype(bf16), "tensor", n_tensor, m).astype(f32)
        return total

    local_count = hidden_in.shape[0]
    hidden = to_relative(hidden_in)
    upstream_local = to_relative(cotangent)
    rows = tokens_full(hidden)

    vectors = jnp.stack([first_gain, first_shift, second_gain, second_shift, dense_bias + down_bias])
    vector_pieces = shuffle(gather_blocks(vectors, "tensor", n_tensor, z_masks), z_masks, z_me)
    vectors = jnp.concatenate(vector_pieces, axis=1)
    n_vec, width = vectors.shape
    packed = jnp.concatenate(
        [vectors.reshape(-1), qkv_bias.reshape(-1).astype(f32), up_bias.reshape(-1).astype(f32)]
    )
    small = packed[None]
    small_order = [0]
    for mask in order_a:
        small = jnp.concatenate([small, swap(small, "dp", n_dp, mask)])
        small_order = small_order + [k ^ mask for k in small_order]
    small = [small[small_order.index(k)] for k in range(n_dp)]
    vec = jnp.concatenate([small[k][: n_vec * width].reshape(n_vec, width) for k in layout_order], axis=1)
    gain_one, shift_one, gain_two, shift_two, out_bias = [vec[i] for i in range(n_vec)]
    bias_at, up_at = n_vec * width, n_vec * width + qkv_bias.size
    true_small = shuffle([s[bias_at:] for s in small], masks, me)
    qkv_flat = jnp.concatenate(
        [s[: qkv_bias.size].reshape(qkv_bias.shape) for s in true_small], axis=1
    ).reshape(-1)
    up_flat = jnp.concatenate(
        [s[up_at - bias_at :].reshape(up_bias.shape) for s in true_small], axis=1
    ).reshape(-1)

    def joined(blocks, axis):
        return jnp.concatenate([blocks[k] for k in layout_order], axis=axis)

    qkv_full = joined(gather_blocks(qkv_weight, "dp", n_dp, order_a), 0)
    up_full = joined(gather_blocks(up_weight, "dp", n_dp, order_b), 0)
    dense_mat = joined(gather_blocks(dense_weight, "dp", n_dp, order_b), 1)
    down_mat = joined(gather_blocks(down_weight, "dp", n_dp, order_a), 1)
    upstream = tokens_full(upstream_local)

    normed, inv_std = norm_stats(rows)
    first = (normed * gain_one + shift_one).astype(bf16)
    second = (normed * gain_two + shift_two).astype(bf16)
    local_normed, local_inv = norm_stats(hidden)
    count = first.shape[0]
    segment, positions = layout(seq_lengths[0], count)
    projected = jnp.dot(first, qkv_full, preferred_element_type=f32) + qkv_flat
    context, log_total, query, keys, values = attend_forward(projected, segment, positions)
    pre_act = jnp.dot(second, up_full, preferred_element_type=f32) + up_flat
    active = gelu_value(pre_act).astype(bf16)
    partial_value = jnp.dot(context, dense_mat, preferred_element_type=f32) + jnp.dot(
        active, down_mat, preferred_element_type=f32
    )
    summed = tokens_sum(partial_value)
    block_out = from_relative((hidden.astype(f32) + summed + out_bias).astype(bf16))

    half = n_dp // 2

    def grad_parts(left, right, axis, order):
        if axis == 0:
            width_half = left.shape[1] // 2
            keep = contract_rows(left[:, :width_half], right)
            send = contract_rows(left[:, width_half:], right).astype(bf16)
        else:
            width_half = right.shape[1] // 2
            keep = contract_rows(left, right[:, :width_half])
            send = contract_rows(left, right[:, width_half:]).astype(bf16)
        keep = dict(zip(layout_order[:half], cut(keep, half, axis)))
        send = dict(zip(layout_order[half:], cut(send, half, axis)))
        return scatter_blocks(keep, send, "dp", n_dp, order)

    back_a, back_b = masks[:1] + high[::-1], masks[:1] + high
    down_shard = grad_parts(active, upstream, 1, back_a)
    dense_shard = grad_parts(context, upstream, 1, back_b)
    grad_pre = contract_cols(upstream, down_mat) * gelu_slope(pre_act)
    up_bias_grad = jnp.sum(grad_pre, axis=0)
    grad_pre_b = grad_pre.astype(bf16)
    up_shard = grad_parts(second, grad_pre_b, 0, back_b)
    grad_second = contract_cols(grad_pre_b, up_full)
    grad_context = contract_cols(upstream, dense_mat).astype(bf16)
    grad_projected = attend_backward(
        query, keys, values, log_total, grad_context, segment, positions
    )
    qkv_bias_grad = jnp.sum(grad_projected, axis=0)
    grad_projected_b = grad_projected.astype(bf16)
    grad_first = contract_cols(grad_projected_b, qkv_full)
    qkv_shard = grad_parts(first, grad_projected_b, 0, back_a)

    grad_normed = tokens_sum(grad_first * gain_one + grad_second * gain_two)
    mean_a = jnp.mean(grad_normed, axis=-1, keepdims=True)
    mean_b = jnp.mean(grad_normed * local_normed, axis=-1, keepdims=True)
    cotangent_f = upstream_local.astype(f32)
    input_grad = from_relative(
        (cotangent_f + local_inv * (grad_normed - mean_a - local_normed * mean_b)).astype(bf16)
    )

    sums = jnp.stack(
        [
            jnp.sum(grad_first * normed, axis=0),
            jnp.sum(grad_first, axis=0),
            jnp.sum(grad_second * normed, axis=0),
            jnp.sum(grad_second, axis=0),
            jnp.sum(cotangent_f, axis=0),
        ]
    )
    sum_pieces = cut(sums, n_dp, 1)
    qkv_pieces = shuffle(
        cut(qkv_bias_grad.reshape(qkv_bias.shape[0], -1), n_dp, 1), masks, me
    )
    up_pieces = shuffle(cut(up_bias_grad.reshape(up_bias.shape[0], -1), n_dp, 1), masks, me)
    blocks = [
        jnp.concatenate(
            [
                sum_pieces[layout_order.index(k)].reshape(-1),
                qkv_pieces[k].reshape(-1),
                up_pieces[k].reshape(-1),
            ]
        )
        for k in range(n_dp)
    ]
    total = sum_blocks(blocks, "dp", n_dp, back_a)
    n_sum = sums.shape[0]
    vec_total = total[: n_sum * width].reshape(n_sum, width)
    rest = total[n_sum * width :]
    qkv_bias_shard = rest[: qkv_bias.size].reshape(qkv_bias.shape)
    up_bias_shard = rest[qkv_bias.size :].reshape(up_bias.shape)
    vec_pieces = shuffle(cut(vec_total, n_tensor, 1), z_masks, z_me)
    vec_mine = sum_blocks(vec_pieces, "tensor", n_tensor, z_masks)
    return (
        block_out,
        input_grad,
        vec_mine[0],
        vec_mine[1],
        vec_mine[2],
        vec_mine[3],
        qkv_shard,
        qkv_bias_shard,
        dense_shard,
        vec_mine[4],
        up_shard,
        up_bias_shard,
        down_shard,
        vec_mine[4],
    )


def solution(mesh):
    placed = (
        P(("dp", "tensor"), None),
        P(("dp", "tensor"), None),
        P("dp", None),
        P(("dp", "tensor")),
        P(("dp", "tensor")),
        P(("dp", "tensor")),
        P(("dp", "tensor")),
        P("dp", "tensor"),
        P("tensor", "dp"),
        P("tensor", "dp"),
        P(("dp", "tensor")),
        P("dp", "tensor"),
        P("tensor", "dp"),
        P("tensor", "dp"),
        P(("dp", "tensor")),
    )
    return jax.shard_map(
        functools.partial(on_device, mesh.shape["dp"], mesh.shape["tensor"]),
        mesh=mesh,
        in_specs=placed,
        out_specs=(
            P(("dp", "tensor"), None),
            P(("dp", "tensor"), None),
            P(("dp", "tensor")),
            P(("dp", "tensor")),
            P(("dp", "tensor")),
            P(("dp", "tensor")),
            P("dp", "tensor"),
            P("tensor", "dp"),
            P("tensor", "dp"),
            P(("dp", "tensor")),
            P("dp", "tensor"),
            P("tensor", "dp"),
            P("tensor", "dp"),
            P(("dp", "tensor")),
        ),
        check_vma=False,
    )
```

```python
import functools
import math

import jax
import jax.numpy as jnp
from jax import lax
from jax.experimental import pallas as pl
from jax.experimental.pallas import tpu as pltpu
from jax.sharding import PartitionSpec as P

HD = 64
ROT = 16
F32, BF16 = jnp.float32, jnp.bfloat16


EPS = 1e-05
ROOT_HALF = 0.7071067811865476
INV_ROOT_TWO_PI = 0.3989422804014327


def gelu_value(pre_act):
    return pre_act * (0.5 * (1.0 + jax.scipy.special.erf(pre_act * ROOT_HALF)))


def gelu_slope(pre_act):
    cumul = 0.5 * (1.0 + jax.scipy.special.erf(pre_act * ROOT_HALF))
    return cumul + pre_act * INV_ROOT_TWO_PI * jnp.exp(-0.5 * pre_act * pre_act)


def layout(lengths, count):
    ends = jnp.cumsum(lengths)
    index = jnp.arange(count, dtype=jnp.int32)
    passed = (index[:, None] >= ends[None, :]).astype(jnp.int32)
    segment = jnp.sum(passed, axis=1)
    start = jnp.sum(passed * lengths[None, :], axis=1)
    return (segment, index - start)


def rotary_tables(positions):
    half = ROT // 2
    freq = 1.0 / 10000.0 ** (jnp.arange(half, dtype=jnp.float32) * (2.0 / ROT))
    angle = positions.astype(jnp.float32)[:, None] * freq[None, :]
    return (jnp.cos(angle)[:, None, :], jnp.sin(angle)[:, None, :])


def rotate(values, cosine, sine):
    half = ROT // 2
    lower = values[..., :half]
    upper = values[..., half:ROT]
    return jnp.concatenate(
        [lower * cosine - upper * sine, upper * cosine + lower * sine, values[..., ROT:]], axis=-1
    )


def rotate_back(grads, cosine, sine):
    half = ROT // 2
    lower = grads[..., :half]
    upper = grads[..., half:ROT]
    return jnp.concatenate(
        [lower * cosine + upper * sine, upper * cosine - lower * sine, grads[..., ROT:]], axis=-1
    )


def score_block(query, keys, segment):
    index = jnp.arange(segment.shape[0], dtype=jnp.int32)
    allowed = (segment[:, None] == segment[None, :]) & (index[None, :] <= index[:, None])
    scores = jnp.einsum("qhd,khd->hqk", query, keys, preferred_element_type=jnp.float32) * HD ** (
        -0.5
    )
    return jnp.where(allowed[None], scores, -jnp.inf)


def attend_forward(projected, segment, positions):
    count = projected.shape[0]
    heads = projected.shape[1] // (3 * HD)
    parts = projected.reshape(count, heads, 3, HD)
    cosine, sine = rotary_tables(positions)
    query = rotate(parts[:, :, 0], cosine, sine).astype(jnp.bfloat16)
    keys = rotate(parts[:, :, 1], cosine, sine).astype(jnp.bfloat16)
    values = parts[:, :, 2].astype(jnp.bfloat16)
    scores = score_block(query, keys, segment)
    row_top = jnp.max(scores, axis=-1, keepdims=True)
    log_total = row_top + jnp.log(jnp.sum(jnp.exp(scores - row_top), axis=-1, keepdims=True))
    prob = jnp.exp(scores - log_total).astype(jnp.bfloat16)
    context = jnp.einsum("hqk,khd->qhd", prob, values, preferred_element_type=jnp.float32)
    return (context.reshape(count, heads * HD).astype(jnp.bfloat16), log_total, query, keys, values)


def attend_backward(query, keys, values, log_total, grad_context, segment, positions):
    count = query.shape[0]
    heads = query.shape[1]
    scores = score_block(query, keys, segment)
    prob_f = jnp.exp(scores - log_total)
    grad_ctx = grad_context.reshape(count, heads, HD)
    grad_prob = jnp.einsum("qhd,khd->hqk", grad_ctx, values, preferred_element_type=jnp.float32)
    delta = jnp.sum(prob_f * grad_prob, axis=-1, keepdims=True)
    grad_score = (prob_f * (grad_prob - delta) * HD ** (-0.5)).astype(jnp.bfloat16)
    grad_query = jnp.einsum("hqk,khd->qhd", grad_score, keys, preferred_element_type=jnp.float32)
    grad_key = jnp.einsum("hqk,qhd->khd", grad_score, query, preferred_element_type=jnp.float32)
    prob_b = prob_f.astype(jnp.bfloat16)
    grad_value = jnp.einsum("hqk,qhd->khd", prob_b, grad_ctx, preferred_element_type=jnp.float32)
    cosine, sine = rotary_tables(positions)
    stacked = jnp.stack(
        [rotate_back(grad_query, cosine, sine), rotate_back(grad_key, cosine, sine), grad_value],
        axis=2,
    )
    return stacked.reshape(count, heads * 3 * HD)


def norm_stats(rows):
    rows_f = rows.astype(jnp.float32)
    mean_row = jnp.mean(rows_f, axis=-1, keepdims=True)
    centred = rows_f - mean_row
    inv_std = lax.rsqrt(jnp.mean(centred * centred, axis=-1, keepdims=True) + EPS)
    return (centred * inv_std, inv_std)


def contract_rows(left, right):
    return lax.dot_general(
        left, right, (((0,), (0,)), ((), ())), preferred_element_type=jnp.float32
    )


def contract_cols(left, right):
    return lax.dot_general(
        left, right, (((1,), (1,)), ((), ())), preferred_element_type=jnp.float32
    )


def on_device(
    hidden_in,
    cotangent,
    seq_lengths,
    first_gain,
    first_shift,
    second_gain,
    second_shift,
    qkv_weight,
    qkv_bias,
    dense_weight,
    dense_bias,
    up_weight,
    up_bias,
    down_weight,
    down_bias,
):
    gain_one, shift_one, gain_two, shift_two, dense_full, down_full = (
        lax.all_gather(first_gain, ("dp", "tensor"), axis=0, tiled=True),
        lax.all_gather(first_shift, ("dp", "tensor"), axis=0, tiled=True),
        lax.all_gather(second_gain, ("dp", "tensor"), axis=0, tiled=True),
        lax.all_gather(second_shift, ("dp", "tensor"), axis=0, tiled=True),
        lax.all_gather(dense_bias, ("dp", "tensor"), axis=0, tiled=True),
        lax.all_gather(down_bias, ("dp", "tensor"), axis=0, tiled=True),
    )
    qkv_full, dense_mat, up_full, down_mat, qkv_bias_full, up_bias_full = (
        lax.all_gather(qkv_weight, "dp", axis=0, tiled=True),
        lax.all_gather(dense_weight, "dp", axis=1, tiled=True),
        lax.all_gather(up_weight, "dp", axis=0, tiled=True),
        lax.all_gather(down_weight, "dp", axis=1, tiled=True),
        lax.all_gather(qkv_bias, "dp", axis=1, tiled=True),
        lax.all_gather(up_bias, "dp", axis=1, tiled=True),
    )
    local_count = hidden_in.shape[0]
    rows = lax.all_gather(hidden_in, "tensor", axis=0, tiled=True)
    normed, inv_std = norm_stats(rows)
    first = (normed * gain_one + shift_one).astype(jnp.bfloat16)
    second = (normed * gain_two + shift_two).astype(jnp.bfloat16)
    offset = lax.axis_index("tensor") * local_count
    local_normed = lax.dynamic_slice_in_dim(normed, offset, local_count, 0)
    local_inv = lax.dynamic_slice_in_dim(inv_std, offset, local_count, 0)
    count = first.shape[0]
    segment, positions = layout(seq_lengths[0], count)
    projected = jnp.dot(
        first, qkv_full, preferred_element_type=jnp.float32
    ) + qkv_bias_full.reshape(-1).astype(jnp.float32)
    context, log_total, query, keys, values = attend_forward(projected, segment, positions)
    pre_act = jnp.dot(second, up_full, preferred_element_type=jnp.float32) + up_bias_full.reshape(
        -1
    ).astype(jnp.float32)
    active = gelu_value(pre_act).astype(jnp.bfloat16)
    partial_value = jnp.dot(context, dense_mat, preferred_element_type=jnp.float32) + jnp.dot(
        active, down_mat, preferred_element_type=jnp.float32
    )
    summed = lax.psum_scatter(
        partial_value.astype(jnp.bfloat16), "tensor", scatter_dimension=0, tiled=True
    ).astype(jnp.float32)
    block_out = (hidden_in.astype(jnp.float32) + summed + dense_full + down_full).astype(
        jnp.bfloat16
    )
    upstream = lax.all_gather(cotangent, "tensor", axis=0, tiled=True)
    qkv_full, dense_mat, up_full, down_mat = (
        lax.all_gather(qkv_weight, "dp", axis=0, tiled=True),
        lax.all_gather(dense_weight, "dp", axis=1, tiled=True),
        lax.all_gather(up_weight, "dp", axis=0, tiled=True),
        lax.all_gather(down_weight, "dp", axis=1, tiled=True),
    )
    down_grad = contract_rows(active, upstream)
    dense_grad = contract_rows(context, upstream)
    grad_pre = contract_cols(upstream, down_mat) * gelu_slope(pre_act)
    up_bias_grad = jnp.sum(grad_pre, axis=0).reshape(up_bias_full.shape)
    grad_pre_b = grad_pre.astype(jnp.bfloat16)
    up_grad = contract_rows(second, grad_pre_b)
    grad_second = contract_cols(grad_pre_b, up_full)
    grad_context = contract_cols(upstream, dense_mat).astype(jnp.bfloat16)
    grad_projected = attend_backward(
        query, keys, values, log_total, grad_context, segment, positions
    )
    qkv_bias_grad = jnp.sum(grad_projected, axis=0).reshape(qkv_bias_full.shape)
    grad_projected_b = grad_projected.astype(jnp.bfloat16)
    qkv_grad = contract_rows(first, grad_projected_b)
    grad_first = contract_cols(grad_projected_b, qkv_full)
    first_rows, second_rows = (
        lax.psum_scatter(
            grad_first.astype(jnp.bfloat16), "tensor", scatter_dimension=0, tiled=True
        ).astype(jnp.float32),
        lax.psum_scatter(
            grad_second.astype(jnp.bfloat16), "tensor", scatter_dimension=0, tiled=True
        ).astype(jnp.float32),
    )
    qkv_shard, dense_shard, up_shard, down_shard, qkv_bias_shard, up_bias_shard = (
        lax.psum_scatter(qkv_grad, "dp", scatter_dimension=0, tiled=True),
        lax.psum_scatter(dense_grad, "dp", scatter_dimension=1, tiled=True),
        lax.psum_scatter(up_grad, "dp", scatter_dimension=0, tiled=True),
        lax.psum_scatter(down_grad, "dp", scatter_dimension=1, tiled=True),
        lax.psum_scatter(qkv_bias_grad, "dp", scatter_dimension=1, tiled=True),
        lax.psum_scatter(up_bias_grad, "dp", scatter_dimension=1, tiled=True),
    )
    grad_normed = first_rows * gain_one + second_rows * gain_two
    mean_a = jnp.mean(grad_normed, axis=-1, keepdims=True)
    mean_b = jnp.mean(grad_normed * local_normed, axis=-1, keepdims=True)
    cotangent_f = cotangent.astype(jnp.float32)
    input_grad = (cotangent_f + local_inv * (grad_normed - mean_a - local_normed * mean_b)).astype(
        jnp.bfloat16
    )
    gain_one_grad, shift_one_grad, gain_two_grad, shift_two_grad, bias_grad = (
        lax.psum_scatter(
            jnp.sum(first_rows * local_normed, axis=0),
            ("dp", "tensor"),
            scatter_dimension=0,
            tiled=True,
        ),
        lax.psum_scatter(
            jnp.sum(first_rows, axis=0), ("dp", "tensor"), scatter_dimension=0, tiled=True
        ),
        lax.psum_scatter(
            jnp.sum(second_rows * local_normed, axis=0),
            ("dp", "tensor"),
            scatter_dimension=0,
            tiled=True,
        ),
        lax.psum_scatter(
            jnp.sum(second_rows, axis=0), ("dp", "tensor"), scatter_dimension=0, tiled=True
        ),
        lax.psum_scatter(
            jnp.sum(cotangent_f, axis=0), ("dp", "tensor"), scatter_dimension=0, tiled=True
        ),
    )
    return (
        block_out,
        input_grad,
        gain_one_grad,
        shift_one_grad,
        gain_two_grad,
        shift_two_grad,
        qkv_shard,
        qkv_bias_shard,
        dense_shard,
        bias_grad,
        up_shard,
        up_bias_shard,
        down_shard,
        bias_grad,
    )


FEW = 8


def powers(count):
    return [1 << b for b in range(count.bit_length() - 1)]


def swap(value, axis, size, mask):
    return lax.ppermute(value, axis, [(i, i ^ mask) for i in range(size)])


def shuffle(pieces, masks, me):
    for mask in masks:
        flip = (me & mask) != 0
        pieces = [jnp.where(flip, pieces[k ^ mask], pieces[k]) for k in range(len(pieces))]
    return pieces


def cut(value, count, axis):
    step = value.shape[axis] // count
    return [lax.slice_in_dim(value, k * step, (k + 1) * step, axis=axis) for k in range(count)]


def gather_blocks(value, axis, size, order):
    if size > FEW:
        stack, names = value[None], [0]
        for mask in order:
            stack = jnp.concatenate([stack, swap(stack, axis, size, mask)])
            names = names + [k ^ mask for k in names]
        return [stack[names.index(k)] for k in range(size)]
    held = {0: value}
    for mask in order:
        held.update({k ^ mask: swap(held[k], axis, size, mask) for k in list(held)})
    return [held[k] for k in range(size)]


def scatter_blocks(keep, send, axis, size, order):
    first = order[0]
    if size > FEW:
        names = list(keep)
        got = swap(jnp.stack([send[k ^ first] for k in names]), axis, size, first)
        stack = jnp.stack([keep[k] for k in names]) + got.astype(jnp.float32)
        for mask in order[1:]:
            stay = [k for k in names if not k & mask]
            away = jnp.stack([stack[names.index(k ^ mask)] for k in stay]).astype(jnp.bfloat16)
            stack = jnp.stack([stack[names.index(k)] for k in stay]) + swap(
                away, axis, size, mask
            ).astype(jnp.float32)
            names = stay
        return stack[0]
    held = {k: keep[k] + swap(send[k ^ first], axis, size, first).astype(jnp.float32) for k in keep}
    for mask in order[1:]:
        held = {
            k: held[k] + swap(held[k ^ mask].astype(jnp.bfloat16), axis, size, mask).astype(jnp.float32)
            for k in held
            if not k & mask
        }
    return held[0]


def sum_blocks(blocks, axis, size, order):
    held = dict(enumerate(blocks))
    for mask in order:
        stay = [k for k in held if not k & mask]
        got = swap(jnp.stack([held[k ^ mask] for k in stay]), axis, size, mask)
        held = {k: held[k] + got[at] for at, k in enumerate(stay)}
    return held[0]


def call(body, outs, args, scratch=(), flops=0, touched=0, scalars=None):
    specs = [pl.BlockSpec(memory_space=pltpu.VMEM) for _ in args]
    if scalars is not None:
        specs = [pl.BlockSpec(memory_space=pltpu.SMEM)] + specs
        args = [scalars] + list(args)
    moved = sum(math.prod(o[0]) * jnp.dtype(o[1]).itemsize for o in outs) + sum(
        a.size * a.dtype.itemsize for a in args
    )
    return pl.pallas_call(
        body,
        out_shape=[jax.ShapeDtypeStruct(*o) for o in outs],
        in_specs=specs,
        out_specs=[pl.BlockSpec(memory_space=pltpu.VMEM) for _ in outs],
        scratch_shapes=list(scratch),
        name=body.func.__name__,
        cost_estimate=pl.CostEstimate(flops=flops, bytes_accessed=moved, transcendentals=0),
    )(*args)


def mm(left, right):
    return jnp.dot(left, right, preferred_element_type=F32)


def mm_nt(left, right):
    return lax.dot_general(left, right, (((1,), (1,)), ((), ())), preferred_element_type=F32)


def transposed(value):
    return jnp.transpose(value.astype(F32)).astype(BF16)


def line_blocks(z, pieces, place):
    own, near, mid, mid_far, end, end_far = pieces
    sources = [
        [own, near, end, end_far],
        [near, own, mid, mid_far],
        [mid_far, mid, own, near],
        [end_far, end, near, own],
    ]
    for at, blocks in enumerate(sources):

        @pl.when(z == at)
        def _(blocks=blocks):
            for j, ref in enumerate(blocks):
                place(j, ref)


def heads_apart(tiles):
    low = lax.broadcasted_iota(jnp.int32, tiles[0].shape, 1) < HD
    out = {}
    for g in range(2):
        t0, t1, t2 = tiles[3 * g : 3 * g + 3]
        out["q", g] = jnp.where(low, t0, t1)
        out["k", g] = jnp.where(low, pltpu.roll(t0, HD, 1), pltpu.roll(t2, HD, 1))
        out["v", g] = jnp.where(low, t1, t2)
    return out


def heads_together(query, key, value):
    low = lax.broadcasted_iota(jnp.int32, query.shape, 1) < HD
    return [
        jnp.where(low, query, pltpu.roll(key, HD, 1)),
        jnp.where(low, value, query),
        jnp.where(low, pltpu.roll(key, HD, 1), value),
    ]


def turn(value, cosine, below, above, sign):
    half = ROT // 2
    width = value.shape[1]
    return (
        value * cosine
        + sign * (pltpu.roll(value, width - half, 1) * below + pltpu.roll(value, half, 1) * above)
    )


def front_kernel(n, scal, *refs):
    pieces, rest = refs[:6], refs[6:]
    vec, bias, cosine, below, above = rest[:5]
    weights, rest = rest[5 : 5 + n], rest[5 + n :]
    first_ref, second_ref, normed_ref, qkv_ref, rows, proj = rest
    count = pieces[0].shape[0]

    def place(j, ref):
        rows[j * count : (j + 1) * count, :] = ref[...]

    line_blocks(scal[1], pieces, place)
    step = 64

    @pl.loop(0, rows.shape[0] // step)
    def _(i):
        at = pl.ds(pl.multiple_of(i * step, step), step)
        x = rows[at, :].astype(F32)
        centred = x - jnp.mean(x, axis=-1, keepdims=True)
        inv = lax.rsqrt(jnp.mean(centred * centred, axis=-1, keepdims=True) + EPS)
        normed = centred * inv
        normed_ref[at, :] = normed.astype(BF16)
        first_ref[at, :] = (normed * vec[0:1, :] + vec[1:2, :]).astype(BF16)
        second_ref[at, :] = (normed * vec[2:3, :] + vec[3:4, :]).astype(BF16)

    wide = 256
    for c in range(qkv_ref.shape[1] // wide):
        at = slice(c * wide, (c + 1) * wide)
        block = jnp.concatenate([w[:, at] for w in weights], axis=0)
        proj[:, at] = mm(first_ref[...], block) + bias[:, at]

    @pl.loop(0, rows.shape[0] // 128)
    def _(i):
        at = pl.ds(pl.multiple_of(i * 128, 128), 128)
        parts = heads_apart([proj[at, t * 128 : (t + 1) * 128] for t in range(6)])
        for (name, g), value in parts.items():
            if name != "v":
                value = turn(value, cosine[at, :], below[at, :], above[at, :], 1.0)
            base = "qkv".index(name) * 256 + g * 128
            qkv_ref[at, base : base + 128] = value.astype(BF16)


def head_lanes(shape, h, axis):
    return (lax.broadcasted_iota(jnp.int32, shape, axis) // HD) == h


def score_t(keys, query_t, start, q_at):
    scores = mm(keys, query_t) * HD ** (-0.5)
    row = lax.broadcasted_iota(jnp.int32, scores.shape, 0)
    col = lax.broadcasted_iota(jnp.int32, scores.shape, 1) + q_at
    return jnp.where((row <= col) & (row >= start), scores, -jnp.inf)


def attend_kernel(wide, qkv, start, context_ref, total_ref, q_t, v_t, c_t):
    count = qkv.shape[0]
    width = context_ref.shape[1]
    q_t[...] = transposed(qkv[:, :width])
    v_t[...] = transposed(qkv[:, 2 * width :])

    @pl.loop(0, width // HD)
    def _(h):
        for at in range(0, count, wide):
            some = at + wide
            query_t = q_t[:, at:some]
            query_t = jnp.where(head_lanes(query_t.shape, h, 0), query_t, jnp.zeros_like(query_t))
            scores = score_t(qkv[:some, width : 2 * width], query_t, start[0:1, at:some], at)
            top = jnp.max(scores, axis=0, keepdims=True)
            prob = jnp.exp(scores - top)
            total = jnp.sum(prob, axis=0, keepdims=True)
            total_ref[pl.ds(h, 1), at:some] = top + jnp.log(total)
            prob_b = (prob * (1.0 / total)).astype(BF16)
            mine = pl.ds(pl.multiple_of(h * HD, HD), HD)
            c_t[mine, at:some] = mm(v_t[mine, :some], prob_b)

    context_ref[...] = jnp.transpose(c_t[...]).astype(BF16)


def upstream_kernel(n, scal, *refs):
    pieces, dense, (full_ref, grad_ref) = refs[:6], refs[6 : 6 + n], refs[6 + n :]
    count = pieces[0].shape[0]
    units = grad_ref.shape[1]

    def place(j, ref):
        full_ref[j * count : (j + 1) * count, :] = ref[...]

    line_blocks(scal[1], pieces, place)
    block = jnp.concatenate([d[d.shape[0] - units :, :] for d in dense], axis=1)
    grad_ref[...] = mm_nt(full_ref[...], block).astype(BF16)


def attend_back_kernel(
    wide, qkv, grad, total, start, cosine, below, above, out_ref, bias_ref, q_t, k_t, g_t, dq_t, dk, dv
):
    count = qkv.shape[0]
    width = grad.shape[1]
    q_t[...] = transposed(qkv[:, :width])
    k_t[...] = transposed(qkv[:, width : 2 * width])
    g_t[...] = transposed(grad[...])
    dk[...] = jnp.zeros_like(dk)
    dv[...] = jnp.zeros_like(dv)

    @pl.loop(0, width // HD)
    def _(h):
        for at in range(0, count, wide):
            some = at + wide

            def one(ref_value, axis):
                keep = head_lanes(ref_value.shape, h, axis)
                return jnp.where(keep, ref_value, jnp.zeros_like(ref_value))

            keys, values = qkv[:some, width : 2 * width], qkv[:some, 2 * width :]
            scores = score_t(keys, one(q_t[:, at:some], 0), start[0:1, at:some], at)
            prob = jnp.exp(scores - total[pl.ds(h, 1), at:some])
            grad_prob = mm(values, one(g_t[:, at:some], 0))
            delta = jnp.sum(prob * grad_prob, axis=0, keepdims=True)
            grad_score = (prob * (grad_prob - delta) * HD ** (-0.5)).astype(BF16)
            mine = pl.ds(pl.multiple_of(h * HD, HD), HD)
            dq_t[mine, at:some] = mm(k_t[mine, :some], grad_score)
            dk[:some, :] += mm(grad_score, one(qkv[at:some, :width], 1))
            dv[:some, :] += mm(prob.astype(BF16), one(grad[at:some, :], 1))

    bias_ref[...] = jnp.zeros_like(bias_ref)
    for i in range(count // 128):
        at = slice(i * 128, (i + 1) * 128)
        for g in range(2):
            lane = slice(g * 128, (g + 1) * 128)
            tables = (cosine[at, :], below[at, :], above[at, :])
            query = turn(jnp.transpose(dq_t[lane, at]), *tables, -1.0)
            key = turn(dk[at, lane], *tables, -1.0)
            for t, tile in enumerate(heads_together(query, key, dv[at, lane])):
                to = slice((3 * g + t) * 128, (3 * g + t + 1) * 128)
                bias_ref[0:1, to] += jnp.sum(tile, axis=0, keepdims=True)
                out_ref[at, to] = tile.astype(BF16)


def up_kernel(n, second, bias, *refs):
    weights, (active_ref, slope_ref) = refs[:n], refs[n:]
    wide = 256
    for c in range(active_ref.shape[1] // wide):
        at = slice(c * wide, (c + 1) * wide)
        block = jnp.concatenate([w[:, at] for w in weights], axis=0)
        pre = mm(second[...], block) + bias[:, at]
        cumul = 0.5 * (1.0 + lax.erf(pre * ROOT_HALF))
        active_ref[:, at] = (pre * cumul).astype(BF16)
        slope_ref[:, at] = cumul + pre * INV_ROOT_TWO_PI * jnp.exp(-0.5 * pre * pre)


def row_parts(scal, acc, at, own_ref, sends):
    z = scal[1]
    count = own_ref.shape[0]
    own_ref[:, at] = acc[pl.ds(pl.multiple_of(z * count, count), count), :]
    for m, ref in enumerate(sends):
        rows = pl.ds(pl.multiple_of((z ^ (m + 1)) * count, count), count)
        ref[:, at] = acc[rows, :].astype(BF16)


def down_rows(low, high):
    return jnp.concatenate([low[...], high[...]], axis=0)


def out_kernel(n, scal, context, active, *refs):
    low, high, rest = refs[:n], refs[n : 2 * n], refs[2 * n :]
    own_ref, s1, s2, s3, acc = rest
    units = active.shape[1]
    heads = context.shape[1]
    for k in range(0, n, 2):
        block = jnp.concatenate(
            [down_rows(low[k], high[k]), down_rows(low[k + 1], high[k + 1])], axis=1
        )
        acc[...] = mm(active[...], block[:units]) + mm(context[...], block[units:])
        wide = low[k].shape[1]
        row_parts(scal, acc, slice(k * wide, (k + 2) * wide), own_ref, (s1, s2, s3))


def pre_kernel(n, upstream, slope, *refs):
    low, high, (out_ref, bias_ref) = refs[:n], refs[n : 2 * n], refs[2 * n :]
    units = slope.shape[1]
    split = low[0].shape[0]
    wide = 256

    def rows(k, a, b):
        if b <= split:
            return low[k][a:b, :]
        if a >= split:
            return high[k][a - split : b - split, :]
        return jnp.concatenate([low[k][a:, :], high[k][: b - split, :]], axis=0)

    for a in range(0, units, wide):
        block = jnp.concatenate([rows(k, a, a + wide) for k in range(n)], axis=1)
        grad = mm_nt(upstream[...], block) * slope[:, a : a + wide]
        bias_ref[0:1, a : a + wide] = jnp.sum(grad, axis=0, keepdims=True)
        out_ref[:, a : a + wide] = grad.astype(BF16)


def normed_grad_kernel(n, scal, grad_proj, grad_pre, normed, vec, *refs):
    qkv, up, rest = refs[:n], refs[n : 2 * n], refs[2 * n :]
    own_ref, s1, s2, s3, sums_ref, acc = rest
    for k in range(0, n, 2):
        wide = qkv[k].shape[0]
        at = slice(k * wide, (k + 2) * wide)
        one = mm_nt(grad_proj[...], jnp.concatenate([qkv[k][...], qkv[k + 1][...]], axis=0))
        two = mm_nt(grad_pre[...], jnp.concatenate([up[k][...], up[k + 1][...]], axis=0))
        base = normed[:, at].astype(F32)
        for i, term in enumerate((one * base, one, two * base, two)):
            sums_ref[i : i + 1, at] = jnp.sum(term, axis=0, keepdims=True)
        acc[...] = one * vec[0:1, at] + two * vec[2:3, at]
        row_parts(scal, acc, at, own_ref, (s1, s2, s3))


def down_grad_kernel(n, active, context, upstream, keep_ref, send_ref, left):
    units = active.shape[1]
    left[:units, :] = transposed(active[...])
    left[units:, :] = transposed(context[...])
    wide = keep_ref.shape[2]
    block = lambda k: upstream[:, k * wide : (k + 1) * wide]
    for i in range(0, n // 2, 2):
        both = mm(left[...], jnp.concatenate([block(2 * i), block(2 * i + 2)], axis=1))
        keep_ref[i] = both[:, :wide]
        keep_ref[i + 1] = both[:, wide:]
        both = mm(left[...], jnp.concatenate([block(2 * i + 1), block(2 * i + 3)], axis=1))
        send_ref[i] = both[:, :wide].astype(BF16)
        send_ref[i + 1] = both[:, wide:].astype(BF16)


def up_grad_kernel(n, second, first, grad_pre, grad_proj, keep_ref, send_ref, left):
    wide = keep_ref.shape[1]
    units = grad_pre.shape[1]
    step = 256
    for source, grad, base in ((second, grad_pre, 0), (first, grad_proj, units)):
        for k in range(n):
            at = (k // 2 + (k % 2) * (n // 2)) * wide
            left[at : at + wide, :] = transposed(source[:, k * wide : (k + 1) * wide])
        for a in range(0, grad.shape[1], step):
            both = mm(left[...], grad[:, a : a + step])
            for i in range(n // 2):
                keep_ref[i, :, base + a : base + a + step] = both[i * wide : (i + 1) * wide]
                low = (n // 2 + i) * wide
                send_ref[i, :, base + a : base + a + step] = both[low : low + wide].astype(BF16)


def line_gather(value):
    move = lambda x, pairs: lax.ppermute(x, "tensor", pairs)
    near = move(value, [(0, 1), (1, 0), (2, 3), (3, 2)])
    mid = move(value, [(1, 2), (2, 1)])
    mid_far = move(near, [(1, 2), (2, 1)])
    end = move(mid, [(1, 0), (2, 3)])
    end_far = move(mid_far, [(1, 0), (2, 3)])
    return [value, near, mid, mid_far, end, end_far]


def block_gather(value, n, x_first):
    near, far = (2, 4) if x_first else (4, 2)
    held = {0: value}
    held[near] = swap(value, "dp", n, near)
    held[far] = swap(value, "dp", n, far)
    held[6] = swap(held[near], "dp", n, far)
    for k in (0, near, far, 6):
        held[k ^ 1] = swap(held[k], "dp", n, 1)
    return [held[k] for k in range(n)]


def block_scatter(keep, send, n, axis):
    got = swap(send, "dp", n, 1)
    size = keep.shape[axis] // 2
    done = []
    for half, (near, far) in enumerate(((2, 4), (4, 2))):
        part = lambda x: lax.slice_in_dim(x, half * size, (half + 1) * size, axis=axis)
        keep_h, got_h = part(keep), part(got)
        term = lambda k: keep_h[k // 2] + got_h[k // 2].astype(F32)
        away = jnp.stack([term(near).astype(BF16), term(near ^ far).astype(BF16)])
        moved = swap(away, "dp", n, near)
        last = swap((term(far) + moved[1].astype(F32)).astype(BF16), "dp", n, far)
        done.append(term(0) + moved[0].astype(F32) + last.astype(F32))
    return jnp.concatenate(done, axis=axis - 1)


def on_blocks(
    n_dp,
    n_tensor,
    hidden_in,
    cotangent,
    seq_lengths,
    first_gain,
    first_shift,
    second_gain,
    second_shift,
    qkv_weight,
    qkv_bias,
    dense_weight,
    dense_bias,
    up_weight,
    up_bias,
    down_weight,
    down_bias,
):
    masks, z_masks = powers(n_dp), powers(n_tensor)
    me, z_me = lax.axis_index("dp"), lax.axis_index("tensor")
    scal = jnp.stack([me, z_me]).astype(jnp.int32)
    local, width = hidden_in.shape
    count = local * n_tensor
    fw = width // n_dp
    heads = qkv_weight.shape[1] // (3 * HD)
    units, hd = up_weight.shape[1], heads * HD

    def relative(value):
        return jnp.concatenate(shuffle(cut(value, n_dp, value.ndim - 1), masks, me), axis=-1)

    vectors = jnp.stack([first_gain, first_shift, second_gain, second_shift, dense_bias + down_bias])
    vectors = jnp.concatenate(
        shuffle(gather_blocks(vectors, "tensor", n_tensor, z_masks), z_masks, z_me), axis=1
    )
    n_vec = vectors.shape[0]
    bias_rows = jnp.concatenate(
        [qkv_bias.astype(F32), up_bias.astype(F32)], axis=1
    )
    packed = jnp.concatenate([vectors.reshape(-1), bias_rows.reshape(-1)])
    small = packed[None]
    names = [0]
    for mask in (2, 4, 1):
        small = jnp.concatenate([small, swap(small, "dp", n_dp, mask)])
        names = names + [k ^ mask for k in names]
    small = [small[names.index(k)] for k in range(n_dp)]
    vec = jnp.concatenate([s[: n_vec * fw].reshape(n_vec, fw) for s in small], axis=1)
    vec = jnp.concatenate([vec, jnp.zeros((8 - n_vec, width), F32)])
    true_bias = shuffle([s[n_vec * fw :].reshape(bias_rows.shape) for s in small], masks, me)
    qb = qkv_bias.shape[1]
    qkv_flat = jnp.concatenate([b[:, :qb] for b in true_bias], axis=1).reshape(1, -1)
    up_flat = jnp.concatenate([b[:, qb:] for b in true_bias], axis=1).reshape(1, -1)

    hidden = relative(hidden_in)
    upstream_local = relative(cotangent)
    hidden_pieces = line_gather(hidden)
    qkv = block_gather(qkv_weight, n_dp, True)
    up = block_gather(up_weight, n_dp, False)
    split = (down_weight.shape[0] + dense_weight.shape[0]) // 2
    low = block_gather(down_weight[:split], n_dp, True)
    high = block_gather(jnp.concatenate([down_weight[split:], dense_weight]), n_dp, False)
    upstream_pieces = line_gather(upstream_local)

    segment, positions = layout(seq_lengths[0], count)
    start = jnp.broadcast_to((jnp.arange(count, dtype=jnp.int32) - positions)[None], (8, count))
    lane = jnp.arange(2 * HD) % HD
    half = ROT // 2
    freq = 1.0 / 10000.0 ** ((lane % half).astype(F32) * (2.0 / ROT))
    angle = positions.astype(F32)[:, None] * freq[None]
    cosine = jnp.where(lane < ROT, jnp.cos(angle), 1.0)
    sine = jnp.sin(angle)
    below = jnp.where(lane < half, -sine, 0.0)
    above = jnp.where((lane >= half) & (lane < ROT), sine, 0.0)

    token = (count, width)
    first, second, normed, qkv_rot = call(
        functools.partial(front_kernel, n_dp),
        [(token, BF16), (token, BF16), (token, BF16), ((count, 3 * hd), BF16)],
        [*hidden_pieces, vec, qkv_flat, cosine, below, above, *qkv],
        [pltpu.VMEM(token, BF16), pltpu.VMEM((count, 3 * hd), F32)],
        2 * count * width * 3 * hd,
        scalars=scal,
    )
    context, total = call(
        functools.partial(attend_kernel, count // 2),
        [((count, hd), BF16), ((8, count), F32)],
        [qkv_rot, start],
        [pltpu.VMEM((hd, count), BF16)] * 2 + [pltpu.VMEM((hd, count), F32)],
        4 * count * count * hd * 4,
    )
    active, slope = call(
        functools.partial(up_kernel, n_dp),
        [((count, units), BF16), ((count, units), F32)],
        [second, up_flat, *up],
        (),
        2 * count * width * units,
    )
    z_parts = [((local, width), F32)] + [((local, width), BF16)] * 3
    z_acc = pltpu.VMEM((count, 2 * fw), F32)
    out_own, *out_send = call(
        functools.partial(out_kernel, n_dp),
        z_parts,
        [context, active, *low, *high],
        [z_acc],
        2 * count * width * (units + hd),
        scalars=scal,
    )
    for m, part in enumerate(out_send):
        out_own = out_own + swap(part, "tensor", n_tensor, m + 1).astype(F32)
    block_out = relative((hidden.astype(F32) + out_own + vec[4]).astype(BF16))

    upstream, grad_context = call(
        functools.partial(upstream_kernel, n_dp),
        [(token, BF16), ((count, hd), BF16)],
        [*upstream_pieces, *high],
        (),
        2 * count * width * hd,
        scalars=scal,
    )
    grad_proj, qkv_bias_grad = call(
        functools.partial(attend_back_kernel, count // 2),
        [((count, 3 * hd), BF16), ((8, 3 * hd), F32)],
        [qkv_rot, grad_context, total, start, cosine, below, above],
        [pltpu.VMEM((hd, count), BF16)] * 3
        + [pltpu.VMEM((hd, count), F32)]
        + [pltpu.VMEM((count, hd), F32)] * 2,
        10 * count * count * hd * 4,
    )
    grad_pre, up_bias_grad = call(
        functools.partial(pre_kernel, n_dp),
        [((count, units), BF16), ((8, units), F32)],
        [upstream, slope, *low, *high],
        (),
        2 * count * width * units,
    )
    dn_own, *rest = call(
        functools.partial(normed_grad_kernel, n_dp),
        z_parts + [((8, width), F32)],
        [grad_proj, grad_pre, normed, vec, *qkv, *up],
        [z_acc],
        2 * count * width * (units + 3 * hd),
        scalars=scal,
    )
    dn_send, sums = rest[:-1], rest[-1]
    keep_d, send_d = call(
        functools.partial(down_grad_kernel, n_dp),
        [((n_dp // 2, units + hd, fw), F32), ((n_dp // 2, units + hd, fw), BF16)],
        [active, context, upstream],
        [pltpu.VMEM((units + hd, count), BF16)],
        2 * count * width * (units + hd),
    )
    keep_u, send_u = call(
        functools.partial(up_grad_kernel, n_dp),
        [((n_dp // 2, fw, units + 3 * hd), F32), ((n_dp // 2, fw, units + 3 * hd), BF16)],
        [second, first, grad_pre, grad_proj],
        [pltpu.VMEM((width, count), BF16)],
        2 * count * width * (units + 3 * hd),
    )
    d_shard = block_scatter(keep_d, send_d, n_dp, 1)
    u_shard = block_scatter(keep_u, send_u, n_dp, 1)
    up_shard, qkv_shard = u_shard[:, :units], u_shard[:, units:]
    down_shard, dense_shard = d_shard[:units], d_shard[units:]

    for m, part in enumerate(dn_send):
        dn_own = dn_own + swap(part, "tensor", n_tensor, m + 1).astype(F32)
    local_normed, local_inv = norm_stats(hidden)
    mean_a = jnp.mean(dn_own, axis=-1, keepdims=True)
    mean_b = jnp.mean(dn_own * local_normed, axis=-1, keepdims=True)
    cotangent_f = upstream_local.astype(F32)
    input_grad = relative(
        (cotangent_f + local_inv * (dn_own - mean_a - local_normed * mean_b)).astype(BF16)
    )

    sums = jnp.concatenate([sums[:4], jnp.sum(cotangent_f, axis=0)[None]])
    n_sum = sums.shape[0]
    held = dict(enumerate(cut(sums, n_dp, 1)))
    biases = jnp.concatenate([qkv_bias_grad[0], up_bias_grad[0]])
    for mask in (1, 2, 4):
        stay = [k for k in held if not k & mask]
        payload = jnp.concatenate([held[k ^ mask].reshape(-1) for k in stay] + [biases])
        got = swap(payload, "dp", n_dp, mask)
        size = n_sum * fw
        held = {
            k: held[k] + got[i * size : (i + 1) * size].reshape(n_sum, fw)
            for i, k in enumerate(stay)
        }
        biases = biases + got[len(stay) * size :]
    qkv_bias_grad = biases[: 3 * hd].reshape(qkv_bias.shape[0], -1)
    up_bias_grad = biases[3 * hd :].reshape(up_bias.shape[0], -1)
    mine = lambda x, n: lax.dynamic_slice_in_dim(x, me * n, n, 1)
    qkv_bias_shard = mine(qkv_bias_grad, qkv_bias.shape[1])
    up_bias_shard = mine(up_bias_grad, up_bias.shape[1])
    vec_pieces = shuffle(cut(held[0], n_tensor, 1), z_masks, z_me)
    vec_mine = sum_blocks(vec_pieces, "tensor", n_tensor, z_masks)
    return (
        block_out,
        input_grad,
        vec_mine[0],
        vec_mine[1],
        vec_mine[2],
        vec_mine[3],
        qkv_shard,
        qkv_bias_shard,
        dense_shard,
        vec_mine[4],
        up_shard,
        up_bias_shard,
        down_shard,
        vec_mine[4],
    )


def solution(mesh):
    n_dp, n_tensor = mesh.shape["dp"], mesh.shape["tensor"]
    blocks = (n_dp, n_tensor) == (8, 4)
    placed = (
        P(("dp", "tensor"), None),
        P(("dp", "tensor"), None),
        P("dp", None),
        P(("dp", "tensor")),
        P(("dp", "tensor")),
        P(("dp", "tensor")),
        P(("dp", "tensor")),
        P("dp", "tensor"),
        P("tensor", "dp"),
        P("tensor", "dp"),
        P(("dp", "tensor")),
        P("dp", "tensor"),
        P("tensor", "dp"),
        P("tensor", "dp"),
        P(("dp", "tensor")),
    )
    return jax.shard_map(
        functools.partial(on_blocks, n_dp, n_tensor) if blocks else on_device,
        mesh=mesh,
        in_specs=placed,
        out_specs=(
            P(("dp", "tensor"), None),
            P(("dp", "tensor"), None),
            P(("dp", "tensor")),
            P(("dp", "tensor")),
            P(("dp", "tensor")),
            P(("dp", "tensor")),
            P("dp", "tensor"),
            P("tensor", "dp"),
            P("tensor", "dp"),
            P(("dp", "tensor")),
            P("dp", "tensor"),
            P("tensor", "dp"),
            P("tensor", "dp"),
            P(("dp", "tensor")),
        ),
        check_vma=False,
    )
```
